32 devices in a mesh: grp: 2 (over x), feat: 8 (over z, y), tok: 2 (over core).
Axes of the slice: x: 2, y: 2, z: 4, core: 2. Of those that a mesh axis runs over, the one named last changes fastest.
Arguments:
- tokens: bfloat16 [2048, 8192], P(('grp', 'tok'), 'feat'), parts along dimension 0, may hold values from -6 to 6
- in_weight: bfloat16 [8192, 3, 8192], P('tok', None, 'feat'), may hold values from -0.0625 to 0.0625
- filters: float32 [512, 128], P('feat'), may hold values from -0.5 to 0.5
- out_weight: bfloat16 [8192, 8192], P('feat'), may hold values from -0.09375 to 0.09375
Outputs:
- mixed_out: bfloat16 [2048, 8192], P(('grp', 'tok'), 'feat'), parts along dimension 0
The draws below stay inside these ranges and needn't reach their ends.
There are 2 independent parts, one for each index of `grp`. The reference program is written for one: setup_inputs(seed, part) draws one part's arguments, and reference() takes and returns one part's arrays. A program takes and returns all parts, laid end to end along the dimension named above; an argument that names none is the same for every part. Nothing has to cross between parts.
All inputs are finite; a program needn't handle non-finite values.
Results may differ from the reference program's by a relative error of at most 0.024.
Values may be sent and summed in bfloat16 or wider, within the bound.
No kernel may reach another device: no remote copies, remote signals or barrier semaphores. Data moves between devices by JAX's collectives and lax.ppermute only.
A program may use at most 192 MiB of HBM per device.

```python
import jax
import jax.numpy as jnp
from jax import lax

D = 8192
KLEN = 128
GROUP = 16
TOKENS = 1024
FILTERS = 512


def with_spikes(array, own_key, source, target, parts, factor):
    def block_of(position):
        return (jnp.arange(array.shape[position]) // (array.shape[position] // parts)).reshape((-1,) + (1,) * (array.ndim - 1 - position))

    first = jax.random.permutation(own_key, parts)[block_of(target)]
    far = (block_of(target) + parts // 2) % parts
    return jnp.where((block_of(source) == first) | (block_of(source) == far), factor * array, array)


def block_scale(rng, dims, cuts, low, top_value):
    factor_of = 1.0
    for position, shards_of in cuts:
        draws = jax.random.uniform(jax.random.fold_in(jax.random.fold_in(rng, 6), position), (shards_of,), jnp.float32, low / len(cuts), top_value / len(cuts))
        factor_of = factor_of * jnp.repeat(jnp.exp(draws), dims[position] // shards_of).reshape((-1,) + (1,) * (len(dims) - 1 - position))
    return factor_of


def normal_values(own_key, dims, scale, limit, cuts=(), held_as=jnp.bfloat16):
    entries = jax.random.normal(own_key, dims, jnp.float32) * scale
    if len(cuts) > 0:
        entries = block_scale(own_key, dims, cuts, -0.22, 0.18) * entries
    return jnp.clip(entries, min=-limit, max=limit).astype(held_as)


def heavy_noise(stream_key, shape, deviation, reach, shards, heavy, kind=jnp.bfloat16):
    result = deviation * jax.random.normal(stream_key, shape, jnp.float32)
    if shards:
        result = result * block_scale(stream_key, shape, shards, -0.22, 0.18)
    return jnp.clip(with_spikes(result, jax.random.fold_in(stream_key, 3), *heavy), -reach, reach).astype(kind)


def setup_inputs(seed: int = 0, part: int = 0) -> dict:
    streams_of = jax.random.split(jax.random.key(seed), 5)
    part_keys = jax.random.split(jax.random.fold_in(streams_of[4], part), 5)
    return {
        "tokens": normal_values(part_keys[0], (TOKENS, D), 1.0, 6.0, ((0, 2), (1, 8))),
        "in_weight": normal_values(streams_of[1], (D, 3, D), D ** -0.5, 0.0625, ((0, 2), (2, 8))),
        "filters": normal_values(streams_of[2], (FILTERS, KLEN), 0.09, 0.5, ((0, 8),), jnp.float32),
        "out_weight": heavy_noise(streams_of[3], (D, D), D ** -0.5, 0.09375, ((0, 8),), (0, 1, 8, 2.0)),
    }


def reference(tokens, in_weight, filters, out_weight):
    count = tokens.shape[0]
    width = tokens.shape[1]
    proj = jnp.dot(tokens, in_weight.reshape(width, 3 * width), preferred_element_type=jnp.float32).astype(jnp.bfloat16)
    proj = proj.reshape(count, 3, width)
    query = proj[:, 0, :].astype(jnp.float32)
    gated = (proj[:, 1, :].astype(jnp.float32) * proj[:, 2, :].astype(jnp.float32)).astype(jnp.bfloat16)
    halo = KLEN - 1
    extended = jnp.concatenate([jnp.zeros((halo, width), jnp.float32), gated.astype(jnp.float32)], axis=0)
    taps = jnp.repeat(filters, GROUP, axis=0).T

    def add_tap(j, total):
        window = lax.dynamic_slice_in_dim(extended, (halo - j).astype(jnp.int32), count, 0)
        coeff = lax.dynamic_index_in_dim(taps, j.astype(jnp.int32), 0, keepdims=True)
        return total + window * coeff

    conv = lax.fori_loop(0, KLEN, add_tap, jnp.zeros((count, width), jnp.float32))
    hidden = (query * conv).astype(jnp.bfloat16)
    return jnp.dot(hidden, out_weight, preferred_element_type=jnp.float32).astype(jnp.bfloat16)
```

```python
import functools

import jax
import jax.numpy as jnp
from jax import lax
from jax.experimental import pallas as pl
from jax.experimental.pallas import tpu as pltpu
from jax.sharding import PartitionSpec as P

GROUP = 16
LANES = 128
BF16 = jnp.bfloat16
F32 = jnp.float32


def across(block):
    n = lax.axis_size("feat")
    return lax.ppermute(block, "feat", [(i, i ^ 1) for i in range(n)])


def onward(block):
    n = lax.axis_size("feat")
    return lax.ppermute(block, "feat", [(i, (i + 2) % n) for i in range(n)])


def toeplitz_body(base_ref, out_ref):
    for i in range(base_ref.shape[0]):
        row = jnp.broadcast_to(base_ref[i : i + 1, :], out_ref.shape[1:])
        out_ref[i] = pltpu.roll(row, 0, 1, stride=1, stride_axis=0).astype(BF16)


def toeplitz(filters):
    n, taps = filters.shape
    base = jnp.pad(filters[:, ::-1], ((0, 0), (1, taps - 1)))
    per = min(8, n)
    return pl.pallas_call(
        toeplitz_body,
        grid=(n // per,),
        in_specs=[pl.BlockSpec((per, 2 * taps), lambda i: (i, 0))],
        out_specs=pl.BlockSpec((per, taps, 2 * taps), lambda i: (i, 0, 0)),
        out_shape=jax.ShapeDtypeStruct((n, taps, 2 * taps), BF16),
        name="toeplitz",
    )(base)


def in_body(slots, table, *refs):
    lhs = refs[:slots]
    own, other, q_ref, g_ref, held, acc, sems = refs[slots:]
    n, k = pl.program_id(0), pl.program_id(1)

    @pl.when((n == 0) & (k == 0))
    def _():
        for i in range(slots):
            pltpu.make_async_copy(lhs[i], held.at[i], sems.at[i]).start()

    @pl.when(n == 0)
    def _():
        pltpu.make_async_copy(lhs[0], held.at[k], sems.at[k]).wait()

    @pl.when(k == 0)
    def _():
        acc[...] = jnp.zeros_like(acc)

    def add(panel):
        block = held[k]
        for s in range(3):
            acc[s] += jnp.dot(block, panel[s], preferred_element_type=F32)

    @pl.when(table[2, k] == 1)
    def _():
        add(own)

    @pl.when(table[2, k] == 0)
    def _():
        add(other)

    @pl.when(k == slots - 1)
    def _():
        q_ref[...] = acc[0].astype(BF16)
        keyed = acc[1].astype(BF16).astype(F32)
        valued = acc[2].astype(BF16).astype(F32)
        g_ref[...] = (keyed * valued).astype(BF16)


def in_project(table, blocks, own, other):
    slots = len(blocks)
    rows, depth = blocks[0].shape
    channels = own.shape[2]
    tile = min(256, channels)
    panel = (3, depth, tile)
    grid = pltpu.PrefetchScalarGridSpec(
        num_scalar_prefetch=1,
        grid=(channels // tile, slots),
        in_specs=[pl.BlockSpec(memory_space=pl.ANY)] * slots
        + [
            pl.BlockSpec(panel, lambda n, k, t: (0, t[0, k], n)),
            pl.BlockSpec(panel, lambda n, k, t: (0, t[1, k], n)),
        ],
        out_specs=[pl.BlockSpec((rows, tile), lambda n, k, t: (0, n))] * 2,
        scratch_shapes=[
            pltpu.VMEM((slots, rows, depth), BF16),
            pltpu.VMEM((3, rows, tile), F32),
            pltpu.SemaphoreType.DMA((slots,)),
        ],
    )
    return pl.pallas_call(
        functools.partial(in_body, slots),
        grid_spec=grid,
        out_shape=[jax.ShapeDtypeStruct((rows, channels), BF16)] * 2,
        cost_estimate=pl.CostEstimate(
            flops=6 * rows * depth * slots * channels,
            bytes_accessed=2 * depth * slots * (rows + 3 * channels),
            transcendentals=0,
        ),
        compiler_params=pltpu.CompilerParams(vmem_limit_bytes=48 << 20),
        name="in_project",
    )(table, *blocks, own, other)


def conv_body(q_ref, g_ref, halo_ref, taps_ref, out_ref):
    per, taps, _ = taps_ref.shape
    rows = g_ref.shape[0]
    stack = taps_ref[...].reshape(per * taps, 2 * taps)
    lane = lax.broadcasted_iota(jnp.int32, (taps, LANES), 1)
    for b in range(rows // taps):
        first = halo_ref[...] if b == 0 else g_ref[(b - 1) * taps : b * taps, :]
        window = jnp.concatenate([first, g_ref[b * taps : (b + 1) * taps, :]], axis=0)
        every = jnp.dot(stack, window, preferred_element_type=F32)
        conv = every[:taps]
        for f in range(1, per):
            conv = jnp.where(lane >= f * GROUP, every[f * taps : (f + 1) * taps], conv)
        query = q_ref[b * taps : (b + 1) * taps, :].astype(F32)
        out_ref[b * taps : (b + 1) * taps, :] = (query * conv).astype(BF16)


def convolve(query, gated, halo, taps):
    rows, channels = gated.shape
    per = LANES // GROUP
    klen = taps.shape[1]
    return pl.pallas_call(
        conv_body,
        grid=(channels // LANES,),
        in_specs=[
            pl.BlockSpec((rows, LANES), lambda i: (0, i)),
            pl.BlockSpec((rows, LANES), lambda i: (0, i)),
            pl.BlockSpec((klen, LANES), lambda i: (0, i)),
            pl.BlockSpec((per, klen, 2 * klen), lambda i: (i, 0, 0)),
        ],
        out_specs=pl.BlockSpec((rows, LANES), lambda i: (0, i)),
        out_shape=jax.ShapeDtypeStruct((rows, channels), BF16),
        cost_estimate=pl.CostEstimate(
            flops=2 * rows * channels * 2 * klen * per,
            bytes_accessed=6 * rows * channels,
            transcendentals=0,
        ),
        name="convolve",
    )(query, gated, halo, taps)


def out_body(columns, h_ref, same_w, cross_w, same_ref, cross_ref):
    same_ref[...] = jnp.dot(h_ref[...], same_w[...], preferred_element_type=F32).astype(BF16)
    cross_ref[...] = jnp.dot(h_ref[...], cross_w[...], preferred_element_type=F32).astype(BF16)


def out_project(columns, hidden, out_weight, width):
    rows, depth = hidden.shape
    tile = min(256, width)
    per = width // tile
    grid = pltpu.PrefetchScalarGridSpec(
        num_scalar_prefetch=1,
        grid=(per,),
        in_specs=[
            pl.BlockSpec((rows, depth), lambda n, t: (0, 0)),
            pl.BlockSpec((depth, tile), lambda n, t: (0, t[0] * per + n)),
            pl.BlockSpec((depth, tile), lambda n, t: (0, t[1] * per + n)),
        ],
        out_specs=[pl.BlockSpec((rows, tile), lambda n, t: (0, n))] * 2,
    )
    return pl.pallas_call(
        out_body,
        grid_spec=grid,
        out_shape=[jax.ShapeDtypeStruct((rows, width), BF16)] * 2,
        cost_estimate=pl.CostEstimate(
            flops=4 * rows * depth * width,
            bytes_accessed=4 * depth * width + 2 * rows * depth + 4 * rows * width,
            transcendentals=0,
        ),
        name="out_project",
    )(columns, hidden, out_weight, out_weight)


def plus(*terms):
    total = terms[0].astype(F32)
    for term in terms[1:]:
        total = total + term.astype(F32)
    return total.astype(BF16)


def shards(tokens, in_weight, filters, out_weight):
    width = tokens.shape[1]
    ring = lax.axis_size("feat") // 2
    me = lax.axis_index("feat")
    tok = lax.axis_index("tok")
    place, side = me // 2, me % 2

    own = jnp.transpose(in_weight, (1, 0, 2))
    other = lax.ppermute(own, "tok", [(0, 1), (1, 0)])
    taps = toeplitz(filters)

    same, cross = [tokens], []
    for k in range(ring):
        cross.append(across(same[k]))
        if k + 1 < ring:
            same.append(onward(same[k]))
    blocks, index = [], []
    for k in range(ring):
        at = (place - k) % ring * 2
        blocks += [same[k], cross[k]]
        index += [at + side, at + 1 - side]
    held = own.shape[1] // width
    local, near, far = [], [], []
    for i in index:
        mine = i // held == tok
        local.append(mine.astype(jnp.int32))
        near.append(jnp.where(mine, i % held, near[-1] if near else 0))
        far.append(jnp.where(mine, far[-1] if far else 0, i % held))
    table = jnp.stack([jnp.stack(near), jnp.stack(far), jnp.stack(local)]).astype(jnp.int32)

    query, gated = in_project(table, blocks, own, other)
    klen = filters.shape[1]
    halo = lax.ppermute(gated[-klen:], "tok", [(0, 1)])
    hidden = convolve(query, gated, halo, taps)

    total = None
    for k in range(1, ring + 1):
        at = (place - k) % ring * 2
        columns = jnp.stack([at + side, at + 1 - side]).astype(jnp.int32)
        mine, theirs = out_project(columns, hidden, out_weight, width)
        terms = [mine, across(theirs)]
        if total is not None:
            terms.append(onward(total))
        total = plus(*terms)
    return total


def solution(mesh):
    in_specs = (P(("grp", "tok"), "feat"), P("tok", None, "feat"), P("feat", None), P("feat", None))
    out_specs = P(("grp", "tok"), "feat")
    return jax.shard_map(shards, mesh=mesh, in_specs=in_specs, out_specs=out_specs, check_vma=False)
```

```python
import functools

import jax
import jax.numpy as jnp
from jax import lax
from jax.experimental import pallas as pl
from jax.experimental.pallas import tpu as pltpu
from jax.sharding import PartitionSpec as P


GROUP = 16
LANES = 128
BF16 = jnp.bfloat16
F32 = jnp.float32


def across(block):
    n = lax.axis_size("feat")
    return lax.ppermute(block, "feat", [(i, i ^ 1) for i in range(n)])


def onward(block):
    n = lax.axis_size("feat")
    return lax.ppermute(block, "feat", [(i, (i + 2) % n) for i in range(n)])


def toeplitz_body(base_ref, out_ref):
    for i in range(base_ref.shape[0]):
        row = jnp.broadcast_to(base_ref[i : i + 1, :], out_ref.shape[1:])
        out_ref[i] = pltpu.roll(row, 0, 1, stride=1, stride_axis=0).astype(BF16)


def toeplitz(filters):
    n, taps = filters.shape
    base = jnp.pad(filters[:, ::-1], ((0, 0), (1, taps - 1)))
    per = min(8, n)
    return pl.pallas_call(
        toeplitz_body,
        grid=(n // per,),
        in_specs=[pl.BlockSpec((per, 2 * taps), lambda i: (i, 0))],
        out_specs=pl.BlockSpec((per, taps, 2 * taps), lambda i: (i, 0, 0)),
        out_shape=jax.ShapeDtypeStruct((n, taps, 2 * taps), BF16),
        name="toeplitz",
    )(base)


def in_body(pieces, first, slots, last, table, *refs):
    refs = list(refs)
    lhs = [refs.pop(0) for _ in pieces]
    own, other = refs.pop(0), refs.pop(0)
    partial = refs.pop(0) if first else None
    outs = [refs.pop(0) for _ in range(2 if last else 1)]
    held, acc, sems = refs
    n, k = pl.program_id(0), pl.program_id(1)

    def copies(slot=None):
        for i, (at, row, rows) in enumerate(pieces):
            if slot is None or at == slot:
                yield pltpu.make_async_copy(lhs[i], held.at[at, pl.ds(row, rows)], sems.at[i])

    @pl.when((n == 0) & (k == 0))
    def _():
        for copy in copies():
            copy.start()

    for slot in range(slots):

        @pl.when((n == 0) & (k == slot))
        def _():
            for copy in copies(slot):
                copy.wait()

    def add(panel, opening):
        block = held[k]
        for s in range(3):
            term = jnp.dot(block, panel[s], preferred_element_type=F32)
            if not opening:
                acc[s] += term
            elif first:
                acc[s] = term + partial[s].astype(F32)
            else:
                acc[s] = term

    for panel, mine in ((own, 1), (other, 0)):
        for opening in (True, False):
            if opening or slots > 1:

                @pl.when((table[2, first + k] == mine) & ((k == 0) == opening))
                def _():
                    add(panel, opening)

    @pl.when(k == slots - 1)
    def _():
        if last:
            outs[0][...] = acc[0].astype(BF16)
            keyed = acc[1].astype(BF16).astype(F32)
            valued = acc[2].astype(BF16).astype(F32)
            outs[1][...] = (keyed * valued).astype(BF16)
        else:
            for s in range(3):
                outs[0][s] = acc[s].astype(BF16)


def in_project(table, first, blocks, own, other, partial=None, last=False):
    slots = len(blocks)
    operands, pieces = [], []
    for slot, block in enumerate(blocks):
        row = 0
        for piece in block if isinstance(block, tuple) else (block,):
            operands.append(piece)
            pieces.append((slot, row, piece.shape[0]))
            row += piece.shape[0]
        rows, depth = row, operands[-1].shape[1]
    channels = own.shape[2]
    tile = min(512, channels)
    panel = (3, depth, tile)
    whole = pl.BlockSpec((3, rows, tile), lambda n, k, t: (0, 0, n))
    flat = pl.BlockSpec((rows, tile), lambda n, k, t: (0, n))
    grid = pltpu.PrefetchScalarGridSpec(
        num_scalar_prefetch=1,
        grid=(channels // tile, slots),
        in_specs=[pl.BlockSpec(memory_space=pl.ANY)] * len(operands)
        + [
            pl.BlockSpec(panel, lambda n, k, t: (0, t[0, first + k], n)),
            pl.BlockSpec(panel, lambda n, k, t: (0, t[1, first + k], n)),
        ]
        + [whole] * bool(first),
        out_specs=[flat, flat] if last else [whole],
        scratch_shapes=[
            pltpu.VMEM((slots, rows, depth), BF16),
            pltpu.VMEM((3, rows, tile), F32),
            pltpu.SemaphoreType.DMA((len(operands),)),
        ],
    )
    flat_shape = jax.ShapeDtypeStruct((rows, channels), BF16)
    out = pl.pallas_call(
        functools.partial(in_body, tuple(pieces), first, slots, last),
        grid_spec=grid,
        out_shape=[flat_shape] * 2 if last else [jax.ShapeDtypeStruct((3, rows, channels), BF16)],
        cost_estimate=pl.CostEstimate(
            flops=6 * rows * depth * slots * channels,
            bytes_accessed=2 * depth * slots * (rows + 3 * channels),
            transcendentals=0,
        ),
        compiler_params=pltpu.CompilerParams(vmem_limit_bytes=48 << 20),
        name="in_project",
    )(table, *operands, own, other, *([partial] if first else []))
    return out if last else out[0]


def conv_body(q_ref, g_ref, halo_ref, taps_ref, out_ref):
    per, taps, _ = taps_ref.shape
    rows = g_ref.shape[0]
    stack = taps_ref[...].reshape(per * taps, 2 * taps)
    lane = lax.broadcasted_iota(jnp.int32, (taps, LANES), 1)
    for b in range(0, rows // taps, 2):
        windows = []
        for at in (b, b + 1):
            first = halo_ref[...] if at == 0 else g_ref[(at - 1) * taps : at * taps, :]
            windows.append(jnp.concatenate([first, g_ref[at * taps : (at + 1) * taps, :]], axis=0))
        every = jnp.dot(stack, jnp.concatenate(windows, axis=1), preferred_element_type=F32)
        for i, at in enumerate((b, b + 1)):
            half = every[:, i * LANES : (i + 1) * LANES]
            conv = half[:taps]
            for f in range(1, per):
                conv = jnp.where(lane >= f * GROUP, half[f * taps : (f + 1) * taps], conv)
            query = q_ref[at * taps : (at + 1) * taps, :].astype(F32)
            out_ref[at * taps : (at + 1) * taps, :] = (query * conv).astype(BF16)


def convolve(query, gated, halo, taps):
    rows, channels = gated.shape
    per = LANES // GROUP
    klen = taps.shape[1]
    return pl.pallas_call(
        conv_body,
        grid=(channels // LANES,),
        in_specs=[
            pl.BlockSpec((rows, LANES), lambda i: (0, i)),
            pl.BlockSpec((rows, LANES), lambda i: (0, i)),
            pl.BlockSpec((klen, LANES), lambda i: (0, i)),
            pl.BlockSpec((per, klen, 2 * klen), lambda i: (i, 0, 0)),
        ],
        out_specs=pl.BlockSpec((rows, LANES), lambda i: (0, i)),
        out_shape=jax.ShapeDtypeStruct((rows, channels), BF16),
        cost_estimate=pl.CostEstimate(
            flops=2 * rows * channels * 2 * klen * per,
            bytes_accessed=6 * rows * channels,
            transcendentals=0,
        ),
        name="convolve",
    )(query, gated, halo, taps)


def out_body(places, pieces, table, h_ref, w_ref, *refs):
    outs, (held, sems) = refs[:-2], refs[-2:]
    j = pl.program_id(0)
    steps = len(places)

    def copies(step):
        for out, row in pieces[step]:
            rows = pl.ds(row, outs[out].shape[0])
            yield pltpu.make_async_copy(held.at[step % 2, rows], outs[out], sems.at[out])

    for step in range(steps):

        @pl.when(j == step)
        def _():
            if step >= 2:
                for copy in copies(step - 2):
                    copy.wait()
            product = jnp.dot(h_ref[...], w_ref[...], preferred_element_type=F32)
            held[step % 2] = product.astype(BF16)
            for copy in copies(step):
                copy.start()
            if step == steps - 1:
                for late in range(max(0, steps - 2), steps):
                    for copy in copies(late):
                        copy.wait()


def out_project(table, places, hidden, out_weight, width):
    rows, depth = hidden.shape
    pieces, shapes = [], []
    for place in places:
        row, here = 0, []
        for part in place[1] if isinstance(place, tuple) else (rows,):
            here.append((len(shapes), row))
            shapes.append(jax.ShapeDtypeStruct((part, width), BF16))
            row += part
        pieces.append(tuple(here))
    places = tuple(place[0] if isinstance(place, tuple) else place for place in places)

    def column(j, t):
        at = t[3, places[0]]
        for step in range(1, len(places)):
            at = jnp.where(j == step, t[3, places[step]], at)
        return 0, at

    steps = len(places)
    grid = pltpu.PrefetchScalarGridSpec(
        num_scalar_prefetch=1,
        grid=(steps,),
        in_specs=[
            pl.BlockSpec((rows, depth), lambda j, t: (0, 0)),
            pl.BlockSpec((depth, width), column),
        ],
        out_specs=[pl.BlockSpec(memory_space=pl.ANY)] * len(shapes),
        scratch_shapes=[
            pltpu.VMEM((2, rows, width), BF16),
            pltpu.SemaphoreType.DMA((len(shapes),)),
        ],
    )
    return pl.pallas_call(
        functools.partial(out_body, places, tuple(pieces)),
        grid_spec=grid,
        out_shape=shapes,
        cost_estimate=pl.CostEstimate(
            flops=2 * rows * depth * width * steps,
            bytes_accessed=2 * steps * width * (depth + rows) + 2 * rows * depth,
            transcendentals=0,
        ),
        name="out_project",
    )(table, hidden, out_weight)


def plus(*terms):
    total = terms[0].astype(F32)
    for term in terms[1:]:
        total = total + term.astype(F32)
    return total.astype(BF16)


def padded(block, above, below):
    return jnp.pad(block, ((above, below), (0, 0)))


def block(tokens, in_weight, filters, out_weight):
    rows, width = tokens.shape
    half = rows // 2
    ring = lax.axis_size("feat") // 2
    me = lax.axis_index("feat")
    tok = lax.axis_index("tok")
    place, side = me // 2, me % 2
    own = jnp.transpose(in_weight, (1, 0, 2))

    held = own.shape[1] // width
    near, far, local, index = [], [], [], []
    for k in range(ring):
        for at in (side, 1 - side):
            i = (place - k) % ring * 2 + at
            mine = i // held == tok
            index.append(i)
            local.append(mine)
            near.append(jnp.where(mine, i % held, near[-1] if near else 0))
            far.append(jnp.where(mine, far[-1] if far else 0, i % held))
    table = jnp.stack([jnp.stack([jnp.asarray(v, jnp.int32) for v in row]) for row in (near, far, local, index)])

    same, cross = [tokens], []
    for k in range(1, ring):
        same.append(onward(same[k - 1]))
        cross.append(across(same[k - 1]))
    cross.append((across(same[-1][:half]), onward(cross[-1][half:])))
    other = lax.ppermute(own, "tok", [(0, 1), (1, 0)])
    taps = toeplitz(filters)

    blocks = [b for pair in zip(same, cross) for b in pair]
    early, late = ring, 2 * ring - 1
    part = in_project(table, 0, blocks[:early], own, other)
    part = in_project(table, early, blocks[early:late], own, other, part)
    query, gated = in_project(table, late, blocks[late:], own, other, part, last=True)
    klen = filters.shape[1]
    halo = lax.ppermute(gated[-klen:], "tok", [(0, 1)])
    hidden = convolve(query, gated, halo, taps)

    upper, lower = out_project(table, [(3, (half, half))], hidden, out_weight, width)
    lower = onward(lower)
    upper = across(upper)
    second = 2 % ring
    mine, next_theirs, next_mine = out_project(
        table, [2, 2 * second + 1, 2 * second], hidden, out_weight, width
    )
    total = onward(plus(mine, padded(upper, 0, half)))
    theirs = across(plus(next_theirs, padded(lower, half, 0)))
    rest = [k % ring for k in range(3, ring + 1)]
    products = out_project(
        table, [p for k in rest for p in (2 * k + 1, 2 * k)], hidden, out_weight, width
    )
    for k in range(2, ring + 1):
        if k > 2:
            theirs = across(products[2 * (k - 3)])
            next_mine = products[2 * (k - 3) + 1]
        total = plus(next_mine, theirs, total)
        if k < ring:
            total = onward(total)
    return total


def solution(mesh):
    in_specs = (P(("grp", "tok"), "feat"), P("tok", None, "feat"), P("feat", None), P("feat", None))
    out_specs = P(("grp", "tok"), "feat")
    return jax.shard_map(block, mesh=mesh, in_specs=in_specs, out_specs=out_specs, check_vma=False)
```
